32 devices in a mesh: parts: 2 (over x), dp: 4 (over y, core), shard: 4 (over z).
Axes of the slice: x: 2, y: 2, z: 4, core: 2. Of those that a mesh axis runs over, the one named last changes fastest.
Arguments:
- projected: bfloat16 [7680, 7680], P(('parts', 'dp', 'shard')), parts along dimension 0, may hold values from -4 to 4
- residual: bfloat16 [7680, 2560], P(('parts', 'dp', 'shard')), parts along dimension 0, may hold values from -6 to 6
- out_weight: bfloat16 [2560, 2560], P(None, 'shard'), may hold values from -0.125 to 0.125
- probe_weight: bfloat16 [2, 2560, 8], replicated, may hold values from -0.125 to 0.125
- labels: int32 [7680], P(('parts', 'dp', 'shard')), parts along dimension 0, may hold values from 0 to 7
- lengths: int32 [32, 9], P(('parts', 'dp', 'shard')), parts along dimension 0, may hold values from 12 to 48, as said below
- destination: int32 [32, 9], P(('parts', 'dp', 'shard')), parts along dimension 0, may hold values from 0 to 3, as said below
Outputs:
- hidden_rows: bfloat16 [18432, 2560], P(('parts', 'dp', 'shard')), parts along dimension 0
- probe_grad: float32 [4, 2560, 8], P('parts'), parts along dimension 0
The draws below stay inside these ranges and needn't reach their ends.
There are 2 independent parts, one for each index of `parts`. The reference program is written for one: setup_inputs(seed, part) draws one part's arguments, and reference() takes and returns one part's arrays. A program takes and returns all parts, laid end to end along the dimension named above; an argument that names none is the same for every part. Nothing has to cross between parts.
Inputs may be any that keep to these rules, and one draw needn't show every extreme that they name: Each row of lengths sums to 240 and holds exactly one protein of length 48. `destination`: A loader assigns at most 3 proteins to any one dp index; in every shard column one dp index is assigned exactly 3 proteins by every loader of that column.
All inputs are finite; a program needn't handle non-finite values.
Results may differ from the reference program's by a relative error of at most 0.0031.
Values may be sent and summed in bfloat16 or wider, within the bound.
No kernel may reach another device: no remote copies, remote signals or barrier semaphores. Data moves between devices by JAX's collectives and lax.ppermute only.
A program may use at most 128 MiB of HBM per device.

```python
import jax
import jax.numpy as jnp
from jax import lax

D = 2560
HS = 128
CLASSES = 8
LMAX = 48
PAIRS = 4
HD = 2560
PROT_DEV = 9
TOK_DEV = 240
LOADERS = 16
TOKENS = 3840
SLOTS = 3
OUT_ROWS = 9216
N_DP = 4
N_SHARD = 4


def draw_projected(key, part):
    return jax.random.truncated_normal(key, -4.0, 4.0, (TOKENS, 3 * HD), jnp.float32).astype(jnp.bfloat16)


def draw_lengths(key, part):
    shortest = LMAX // 4
    paired = jax.random.randint(jax.random.fold_in(key, 11), (LOADERS, PAIRS), shortest, LMAX - shortest + 1)
    pieces = jnp.concatenate([jnp.full((LOADERS, 1), LMAX, jnp.int32), paired.astype(jnp.int32), (LMAX - paired).astype(jnp.int32)], axis=1)
    order_keys = jax.random.split(jax.random.fold_in(key, 12), LOADERS)

    def shuffle_row(row_key):
        return jax.random.permutation(row_key, PROT_DEV)
    orders = jax.vmap(shuffle_row)(order_keys)
    return jnp.take_along_axis(pieces, orders, axis=1).astype(jnp.int32)


def draw_destination(key, part):
    slot_count = (PROT_DEV + N_DP - 1) // N_DP
    favored = jax.random.randint(jax.random.fold_in(key, 21), (N_SHARD,), 0, N_DP).astype(jnp.int32)
    row_keys = jax.random.split(jax.random.fold_in(key, 22), LOADERS)

    def one_row(row_key, loader):
        target = favored[loader % N_SHARD]
        drawn = jax.random.permutation(jax.random.fold_in(row_key, 1), (N_DP - 1) * slot_count)[:PROT_DEV - slot_count] // slot_count
        others = (drawn + (drawn >= target).astype(jnp.int32)).astype(jnp.int32)
        listed = jnp.concatenate([jnp.full((slot_count,), target, jnp.int32), others])
        shuffle = jax.random.permutation(jax.random.fold_in(row_key, 2), PROT_DEV)
        return listed[shuffle]
    return jax.vmap(one_row)(row_keys, jnp.arange(LOADERS, dtype=jnp.int32)).astype(jnp.int32)


def with_ends(result, own_key, low, largest):
    spot = [jax.random.randint(jax.random.fold_in(own_key, axis), (), 0, length) for axis, length in enumerate(result.shape)]
    widest = result.shape.index(max(result.shape))
    neighbour = spot[:widest] + [(spot[widest] + 1) % result.shape[widest]] + spot[widest + 1:]
    return result.at[tuple(spot)].set(low).at[tuple(neighbour)].set(largest)


def shard_levels(stream_key, dims, shards, least, high):
    factor_of = 1.0
    for dim, shards_of in shards:
        heights = jax.random.uniform(jax.random.fold_in(jax.random.fold_in(stream_key, 6), dim), (shards_of,), jnp.float32, least / len(shards), high / len(shards))
        factor_of = factor_of * jnp.repeat(jnp.exp(heights), dims[dim] // shards_of).reshape((-1,) + (1,) * (len(dims) - 1 - dim))
    return factor_of


def gaussian(rng, extent, width, most, cuts=(), kind=jnp.bfloat16):
    loudness = shard_levels(rng, extent, cuts, -0.22, 0.18) if cuts else 1.0
    values = jax.random.normal(rng, extent, jnp.float32) * width * loudness
    return jnp.minimum(jnp.maximum(values, -most), most).astype(kind)


def setup_inputs(seed: int = 0, part: int = 0) -> dict:
    key_of = jax.random.split(jax.random.key(seed), 8)
    part_keys = jax.random.split(jax.random.fold_in(key_of[7], part), 8)
    return {
        "projected": draw_projected(jax.random.fold_in(jax.random.fold_in(key_of[7], part), 71), part),
        "residual": gaussian(part_keys[1], (TOKENS, D), 1.0, 6.0, ((0, 16),)),
        "out_weight": gaussian(key_of[2], (HD, D), HD ** -0.5, 0.125, ((1, 4),)),
        "probe_weight": gaussian(key_of[3], (2, D, CLASSES), D ** -0.5, 0.125),
        "labels": with_ends(jax.random.randint(part_keys[4], (TOKENS,), 0, CLASSES), jax.random.fold_in(part_keys[4], 1), 0, CLASSES - 1).astype(jnp.int32),
        "lengths": draw_lengths(jax.random.fold_in(jax.random.fold_in(key_of[7], part), 71), part),
        "destination": draw_destination(jax.random.fold_in(jax.random.fold_in(key_of[7], part), 71), part),
    }


def attend(blocks, block_lengths):
    block_count = blocks.shape[0]
    span_rows = blocks.shape[1]
    head_width = blocks.shape[2] // 3
    head_count = head_width // HS
    queries = blocks[:, :, :head_width].reshape(block_count, span_rows, head_count, HS).astype(jnp.float32)
    key_rows = blocks[:, :, head_width:2 * head_width].reshape(block_count, span_rows, head_count, HS).astype(jnp.float32)
    value_rows = blocks[:, :, 2 * head_width:].reshape(block_count, span_rows, head_count, HS).astype(jnp.float32)
    scores = jnp.einsum('plhs,pmhs->phlm', queries, key_rows) * (HS ** -0.5)
    keep_mask = (jnp.arange(span_rows, dtype=jnp.int32)[None, :] < block_lengths[:, None]).astype(jnp.float32)
    weights = jnp.exp(scores) * keep_mask[:, None, None, :]
    denominator = jnp.sum(weights, axis=-1, keepdims=True) + (block_lengths == 0).astype(jnp.float32)[:, None, None, None]
    weight_low = lax.optimization_barrier((weights / denominator).astype(jnp.bfloat16))
    attended = jnp.einsum('phlm,pmhs->plhs', weight_low.astype(jnp.float32), value_rows)
    return attended.reshape(block_count * span_rows, head_width).astype(jnp.bfloat16)


def probe_terms(represent_x, represent_h, label_rows, keep_mask, probe_weight):
    one_hot = (label_rows[:, None] == jnp.arange(CLASSES, dtype=jnp.int32)[None, :]).astype(jnp.float32)
    collected = []
    for which, represent in enumerate((represent_x, represent_h)):
        logits = jnp.dot(represent, probe_weight[which], preferred_element_type=jnp.float32)
        exponent = jnp.exp(logits)
        likelihood = exponent / jnp.sum(exponent, axis=1, keepdims=True)
        mismatch = ((likelihood - one_hot) * keep_mask[:, None] / TOK_DEV).astype(jnp.bfloat16)
        collected.append(lax.dot_general(represent, mismatch, (((0,), (0,)), ((), ())), preferred_element_type=jnp.float32))
    return jnp.stack(collected)


def reference(projected, residual, out_weight, probe_weight, labels, lengths, destination):
    offsets = jnp.arange(LMAX, dtype=jnp.int32)

    def one_loader(loader):
        own_lengths = lengths[loader]
        starts = (jnp.cumsum(own_lengths) - own_lengths).astype(jnp.int32)
        row_index = (jnp.minimum(starts[:, None] + offsets[None, :], TOK_DEV - 1) + loader * TOK_DEV).reshape(-1).astype(jnp.int32)
        keep_mask = (offsets[None, :] < own_lengths[:, None]).astype(jnp.float32).reshape(-1)
        blocks = jnp.take(projected, row_index, axis=0).reshape(PROT_DEV, LMAX, 3 * HD)
        attended = attend(blocks, own_lengths)
        represent = jnp.where(keep_mask[:, None] > 0, jnp.take(residual, row_index, axis=0), 0).astype(jnp.bfloat16)
        mixed_rows = jnp.dot(attended, out_weight, preferred_element_type=jnp.float32) + represent.astype(jnp.float32)
        hidden = (mixed_rows * keep_mask[:, None]).astype(jnp.bfloat16)
        own_labels = jnp.take(labels, row_index)
        grad_terms = probe_terms(represent, hidden, own_labels, keep_mask, probe_weight)
        return hidden.reshape(PROT_DEV, LMAX, D), grad_terms

    hidden_all, grad_terms = lax.map(one_loader, jnp.arange(LOADERS, dtype=jnp.int32))
    positions = jnp.arange(PROT_DEV, dtype=jnp.int32)
    same_dest = destination[:, :, None] == destination[:, None, :]
    before = positions[None, :, None] > positions[None, None, :]
    slot_rank = jnp.sum((same_dest & before).astype(jnp.int32), axis=2).astype(jnp.int32)
    loader_ids = jnp.arange(LOADERS, dtype=jnp.int32)
    source = loader_ids // N_SHARD
    column = loader_ids % N_SHARD
    receiver = destination * N_SHARD + column[:, None]
    block_index = ((receiver * N_DP + source[:, None]) * SLOTS + slot_rank).astype(jnp.int32)
    placed = jnp.zeros((LOADERS * N_DP * SLOTS, LMAX, D), jnp.bfloat16)
    placed = placed.at[block_index.reshape(-1)].set(hidden_all.reshape(LOADERS * PROT_DEV, LMAX, D))
    return placed.reshape(OUT_ROWS, D), jnp.sum(grad_terms, axis=0)
```

```python
import functools

import jax
import jax.numpy as jnp
from jax import lax
from jax.experimental import pallas as pl
from jax.experimental.pallas import tpu as pltpu
from jax.sharding import PartitionSpec as P

HS = 128
CLASSES = 8
LMAX = 48
LANES = 128

VMEM = pl.BlockSpec(memory_space=pltpu.VMEM)
SMEM = pl.BlockSpec(memory_space=pltpu.SMEM)
ANY = pl.BlockSpec(memory_space=pl.ANY)


def is_pow2(n):
    return n & (n - 1) == 0


def aligned(value, unit):
    return pl.multiple_of(value, unit)


def attention_kernel(
    prot_count, slot_count, group, len_ref, dest_ref, me_ref, q_ref, k_ref, v_ref, att_ref, sel_ref, mask_ref
):
    rows = q_ref.shape[0]

    @pl.when(pl.program_id(0) == 0)
    def _():
        starts = []
        total = 0
        for p in range(prot_count):
            starts.append(total)
            total = total + len_ref[p]
        row = lax.broadcasted_iota(jnp.int32, (rows, rows), 0)
        col = lax.broadcasted_iota(jnp.int32, (rows, rows), 1)
        row_low, row_high = jnp.zeros_like(row), jnp.zeros_like(row)
        for p in range(prot_count):
            inside = (row >= starts[p]) & (row < starts[p] + len_ref[p])
            row_low = jnp.where(inside, starts[p], row_low)
            row_high = jnp.where(inside, starts[p] + len_ref[p], row_high)
        mask_ref[...] = ((col >= row_low) & (col < row_high)).astype(jnp.float32)

        ranks = []
        for p in range(prot_count):
            rank = 0
            for q in range(p):
                rank = rank + (dest_ref[q] == dest_ref[p]).astype(jnp.int32)
            ranks.append(rank)
        t_row = lax.broadcasted_iota(jnp.int32, (LMAX, rows), 0)
        t_col = lax.broadcasted_iota(jnp.int32, (LMAX, rows), 1)
        me = me_ref[0]
        for j in range(group):
            target = peer(me, j, group)
            for r in range(slot_count):
                start, length = jnp.int32(0), jnp.int32(0)
                for p in range(prot_count):
                    hit = (dest_ref[p] == target) & (ranks[p] == r)
                    start = jnp.where(hit, starts[p], start)
                    length = jnp.where(hit, len_ref[p], length)
                chosen = (t_col == t_row + start) & (t_row < length)
                block = (j * slot_count + r) * LMAX
                sel_ref[block : block + LMAX, :] = chosen.astype(jnp.float32).astype(jnp.bfloat16)

    for h in range(q_ref.shape[1] // HS):
        cols = slice(h * HS, (h + 1) * HS)
        scores = lax.dot_general(
            q_ref[:, cols], k_ref[:, cols], (((1,), (1,)), ((), ())), preferred_element_type=jnp.float32
        ) * HS ** (-0.5)
        weights = jnp.where(mask_ref[...] > 0, jnp.exp(scores), 0.0)
        total = jnp.sum(weights, axis=1, keepdims=True)
        low = (weights / total).astype(jnp.bfloat16)
        att_ref[:, cols] = jnp.dot(low, v_ref[:, cols], preferred_element_type=jnp.float32).astype(jnp.bfloat16)


def attention(projected, lengths, destination, me, group, slot_count):
    rows, width = projected.shape
    hidden = width // 3
    per = 4 * HS if hidden % (4 * HS) == 0 else HS
    steps = hidden // per
    prot_count = lengths.shape[0]
    sel_rows = group * slot_count * LMAX
    return pl.pallas_call(
        functools.partial(attention_kernel, prot_count, slot_count, group),
        grid_spec=pltpu.PrefetchScalarGridSpec(
            num_scalar_prefetch=3,
            grid=(steps,),
            in_specs=[
                pl.BlockSpec((rows, per), lambda i, *_: (0, i)),
                pl.BlockSpec((rows, per), lambda i, *_: (0, i + steps)),
                pl.BlockSpec((rows, per), lambda i, *_: (0, i + 2 * steps)),
            ],
            out_specs=[
                pl.BlockSpec((rows, per), lambda i, *_: (0, i)),
                pl.BlockSpec((sel_rows, rows), lambda i, *_: (0, 0)),
            ],
            scratch_shapes=[pltpu.VMEM((rows, rows), jnp.float32)],
        ),
        out_shape=[
            jax.ShapeDtypeStruct((rows, hidden), jnp.bfloat16),
            jax.ShapeDtypeStruct((sel_rows, rows), jnp.bfloat16),
        ],
        name="attention",
    )(lengths, destination, me, projected, projected, projected)


def project_kernel(piece_count, group, where_ref, att_ref, resid_ref, sel_ref, *refs):
    pieces, (hid_ref, *send_refs) = refs[:piece_count], refs[piece_count:]
    width = hid_ref.shape[1]
    total = None
    for i, piece in enumerate(pieces):
        depth = piece.shape[0]
        if piece_count == 1:
            rows = att_ref[...]
        else:
            rows = att_ref[:, pl.ds(aligned(where_ref[1 + i], LANES), depth)]
        part = jnp.dot(rows, piece[...], preferred_element_type=jnp.float32)
        total = part if total is None else total + part
    if resid_ref.shape[1] == width:
        resid = resid_ref[...]
    else:
        resid = resid_ref[:, pl.ds(aligned(where_ref[0], LANES), width)]
    hid_ref[...] = (total + resid.astype(jnp.float32)).astype(jnp.bfloat16)
    span = sel_ref.shape[0] // group
    for j, send in enumerate(send_refs):
        send[...] = jnp.dot(
            sel_ref[j * span : (j + 1) * span, :], hid_ref[...], preferred_element_type=jnp.float32
        ).astype(jnp.bfloat16)


def project(where, att, resid, sel, pieces, group):
    rows, width = att.shape[0], pieces[0].shape[1]
    span = sel.shape[0] // group
    return pl.pallas_call(
        functools.partial(project_kernel, len(pieces), group),
        in_specs=[SMEM] + [VMEM] * (3 + len(pieces)),
        out_specs=[VMEM] * (1 + group),
        out_shape=[jax.ShapeDtypeStruct((rows, width), jnp.bfloat16)]
        + [jax.ShapeDtypeStruct((span, width), jnp.bfloat16)] * group,
        name="project",
    )(where, att, resid, sel, *pieces)


def probe_kernel(chunk_widths, tok_count, where_ref, label_ref, probe_ref, *refs):
    chunks, grad_ref = refs[: len(chunk_widths)], refs[len(chunk_widths)]
    logits = None
    for i, chunk in enumerate(chunks):
        cols = pl.ds(aligned(where_ref[i], LANES), chunk_widths[i]) if len(chunks) > 1 else slice(None)
        part = lax.dot_general(
            probe_ref[:, cols], chunk[...], (((1,), (1,)), ((), ())), preferred_element_type=jnp.float32
        )
        logits = part if logits is None else logits + part
    exponent = jnp.exp(logits)
    likelihood = exponent / jnp.sum(exponent, axis=0, keepdims=True)
    one_hot = (lax.broadcasted_iota(jnp.int32, logits.shape, 0) == label_ref[...]).astype(jnp.float32)
    mismatch = ((likelihood - one_hot) / tok_count).astype(jnp.bfloat16)
    for i, chunk in enumerate(chunks):
        cols = pl.ds(aligned(where_ref[i], LANES), chunk_widths[i]) if len(chunks) > 1 else slice(None)
        grad_ref[:, cols] = jnp.dot(mismatch, chunk[...], preferred_element_type=jnp.float32)


def probe_grad(where, labels, probe, chunks):
    tok_count = labels.shape[1]
    return pl.pallas_call(
        functools.partial(probe_kernel, tuple(c.shape[1] for c in chunks), tok_count),
        in_specs=[SMEM] + [VMEM] * (2 + len(chunks)),
        out_specs=VMEM,
        out_shape=jax.ShapeDtypeStruct(probe.shape, jnp.float32),
        name="probe",
    )(where, labels, probe, *chunks)


def place_kernel(count, width, where_ref, *refs):
    out_ref, sems = refs[-2], refs[-1]
    copies = []
    for j in range(count):
        span = refs[j].shape[0]
        copies.append(
            pltpu.make_async_copy(
                refs[j],
                out_ref.at[
                    pl.ds(aligned(where_ref[1 + j] * span, 16), span),
                    pl.ds(aligned(where_ref[0], LANES), width),
                ],
                sems.at[j],
            )
        )
    for copy in copies:
        copy.start()
    for copy in copies:
        copy.wait()


def place(where, blocks, out, shape):
    count, width = len(blocks), blocks[0].shape[1]
    held = [] if out is None else [out]
    return pl.pallas_call(
        functools.partial(place_kernel, count, width),
        in_specs=[SMEM] + [ANY] * (count + len(held)),
        out_specs=ANY,
        out_shape=jax.ShapeDtypeStruct(shape, jnp.bfloat16),
        scratch_shapes=[pltpu.SemaphoreType.DMA((count,))],
        input_output_aliases={1 + count: 0} if held else {},
        name="place",
    )(where, *blocks, *held)


def peer(me, j, n):
    return me ^ j if is_pow2(n) else lax.rem(me + j, n)


def source(me, j, n):
    return me ^ j if is_pow2(n) else lax.rem(me + n - j, n)


def swap(x, axis, j):
    n = lax.axis_size(axis)
    return lax.ppermute(x, axis, [(i, int(i ^ j) if is_pow2(n) else (i + j) % n) for i in range(n)])


def tree_sum(terms):
    while len(terms) > 1:
        terms = [a + b for a, b in zip(terms[::2], terms[1::2])]
    return terms[0]


def sum_over_group(x, me):
    group, ring = lax.axis_size("dp"), lax.axis_size("shard")
    piece = x.shape[1] // group
    if group > 4 or not (is_pow2(group) and is_pow2(ring)) or x.shape[1] % group:
        return lax.psum(x, ("dp", "shard"))

    def cut(j):
        return lax.dynamic_slice(x, (0, (me ^ j) * piece), (x.shape[0], piece))

    mine = tree_sum([cut(0)] + [swap(cut(j), "dp", j) for j in range(1, group)])
    mine = tree_sum([mine] + [swap(mine, "shard", j) for j in range(1, ring)])
    total = jnp.zeros_like(x)
    for j in range(group):
        part = swap(mine, "dp", j) if j else mine
        total = lax.dynamic_update_slice(total, part, (0, (me ^ j) * piece))
    return total


def per_device(projected, residual, out_weight, probe_weight, labels, lengths, destination):
    group, ring, parts = lax.axis_size("dp"), lax.axis_size("shard"), lax.axis_size("parts")
    me = lax.axis_index("dp").astype(jnp.int32)
    z = lax.axis_index("shard").astype(jnp.int32)
    x = lax.axis_index("parts").astype(jnp.int32)
    slot_count = -(-lengths.shape[1] // group)
    inner, columns = out_weight.shape
    hidden_width = residual.shape[1]
    rows_out = group * slot_count * LMAX

    cores = 2 if group > 1 and is_pow2(group) else 1
    pairs = 2 if parts == 2 else 1
    shares = pairs * cores
    depth = inner // shares
    mine = (x % pairs) * cores + me % cores
    easy = columns % LANES == 0 and depth % LANES == 0
    splits = SPLITS if easy and sum(SPLITS) == columns else (columns,)

    ring_next = [(i, (i + 1) % ring) for i in range(ring)]
    offsets = [sum(splits[:i]) for i in range(len(splits))]
    held = [
        lax.dynamic_slice(out_weight, (mine * depth, off), (depth, width))
        for off, width in zip(offsets, splits)
    ]

    own_scalar = me.reshape(1)
    att, sel = attention(projected, lengths[0], destination[0], own_scalar, group, slot_count)
    label_row = labels.reshape(1, -1)
    probes = jnp.swapaxes(probe_weight, 1, 2)
    zero = jnp.zeros((1,), jnp.int32)
    grad_first = sum_over_group(probe_grad(zero, label_row, probes[0], [residual]), me)

    out = None
    hidden_chunks, hidden_where = [], []

    def finish(step, off, pieces, piece_rows, out):
        width = pieces[0].shape[1]
        col = lax.rem(z + ring - step, ring) * columns + off
        resid = residual if easy else lax.dynamic_slice(residual, (0, col), (residual.shape[0], width))
        where = jnp.stack([col] + [r * depth for r in piece_rows])
        hid, *sends = project(where, att, resid, sel, pieces, group)
        hidden_chunks.append(hid)
        hidden_where.append(col)
        if group <= 4:
            blocks = [sends[0]] + [swap(s, "dp", j) for j, s in enumerate(sends) if j]
        else:
            packed = jnp.stack(sends)
            order = jnp.stack([peer(me, j, group) for j in range(group)])
            packed = jnp.zeros_like(packed).at[order].set(packed)
            packed = lax.all_to_all(packed, "dp", split_axis=0, concat_axis=0, tiled=True)
            blocks = [packed[source(me, j, group)] for j in range(group)]
        if easy:
            spots = jnp.stack([col] + [source(me, j, group) for j in range(group)])
            return place(spots, blocks, out, (rows_out, hidden_width))
        if out is None:
            out = jnp.zeros((rows_out, hidden_width), jnp.bfloat16)
        for j, block in enumerate(blocks):
            out = lax.dynamic_update_slice(out, block, (source(me, j, group) * block.shape[0], col))
        return out

    out = finish(0, 0, [out_weight], [jnp.int32(0)], out)
    for step in range(1, ring):
        for i, off in enumerate(offsets):
            held[i] = lax.ppermute(held[i], "shard", ring_next)
            pieces, piece_rows = [held[i]], [mine]
            if pairs == 2:
                pieces.append(lax.ppermute(held[i], "parts", [(0, 1), (1, 0)]))
                piece_rows.append(mine ^ cores)
            if cores == 2:
                pieces += [swap(p, "dp", 1) for p in list(pieces)]
                piece_rows += [r ^ 1 for r in piece_rows]
            out = finish(step, off, pieces, piece_rows, out)
    if easy:
        grad_second = probe_grad(jnp.stack(hidden_where), label_row, probes[1], hidden_chunks)
    else:
        full = jnp.zeros((residual.shape[0], hidden_width), jnp.bfloat16)
        for col, chunk in zip(hidden_where, hidden_chunks):
            full = lax.dynamic_update_slice(full, chunk, (0, col))
        grad_second = probe_grad(zero, label_row, probes[1], [full])
    grad_second = sum_over_group(grad_second, me)
    return out, jnp.swapaxes(jnp.stack([grad_first, grad_second]), 1, 2)


SPLITS = (384, 256)


def solution(mesh):
    return jax.shard_map(
        per_device,
        mesh=mesh,
        in_specs=(
            P(("parts", "dp", "shard"), None),
            P(("parts", "dp", "shard"), None),
            P(None, "shard"),
            P(),
            P(("parts", "dp", "shard")),
            P(("parts", "dp", "shard"), None),
            P(("parts", "dp", "shard"), None),
        ),
        out_specs=(P(("parts", "dp", "shard"), None), P("parts", None, None)),
        check_vma=False,
    )
```

```python
import functools

import jax
import jax.numpy as jnp
from jax import lax
from jax.experimental import pallas as pl
from jax.experimental.pallas import tpu as pltpu
from jax.sharding import PartitionSpec as P

HS = 128
CLASSES = 8
LMAX = 48
LANES = 128
PARTS_OF_COLUMNS = (3, 2)

VMEM = pl.BlockSpec(memory_space=pltpu.VMEM)
ANY = pl.BlockSpec(memory_space=pl.ANY)
SMALL = pltpu.CompilerParams(vmem_limit_bytes=12 * 2**20)
F32, BF16, I32 = jnp.float32, jnp.bfloat16, jnp.int32
NT = (((1,), (1,)), ((), ()))


def near(x):
    return pltpu.with_memory_space_constraint(x, pltpu.VMEM)


def is_pow2(n):
    return n & (n - 1) == 0


def lanes_at(start, width):
    return pl.ds(pl.multiple_of(start, LANES), width)


def peer(me, j, n):
    return me ^ j if is_pow2(n) else lax.rem(me + j, n)


def source(me, j, n):
    return me ^ j if is_pow2(n) else lax.rem(me + n - j, n)


def mismatch_of(logits, label_row, tok_count):
    exponent = jnp.exp(logits)
    likelihood = exponent / jnp.sum(exponent, axis=0, keepdims=True)
    one_hot = (lax.broadcasted_iota(I32, logits.shape, 0) == label_row).astype(F32)
    return ((likelihood - one_hot) / tok_count).astype(BF16)


def attention_kernel(
    prot_count, slot_count, group, len_ref, dest_ref, q_ref, k_ref, v_ref, att_ref, sel_ref, mask_ref
):
    rows = q_ref.shape[0]

    @pl.when(pl.program_id(0) == 0)
    def _():
        starts = []
        total = 0
        for p in range(prot_count):
            starts.append(total)
            total = total + len_ref[p]
        row = lax.broadcasted_iota(I32, (rows, rows), 0)
        col = lax.broadcasted_iota(I32, (rows, rows), 1)
        row_low, row_high = jnp.zeros_like(row), jnp.zeros_like(row)
        for p in range(prot_count):
            inside = (row >= starts[p]) & (row < starts[p] + len_ref[p])
            row_low = jnp.where(inside, starts[p], row_low)
            row_high = jnp.where(inside, starts[p] + len_ref[p], row_high)
        mask_ref[...] = ((col >= row_low) & (col < row_high)).astype(F32)

        ranks = []
        for p in range(prot_count):
            rank = 0
            for q in range(p):
                rank = rank + (dest_ref[q] == dest_ref[p]).astype(I32)
            ranks.append(rank)
        t_row = lax.broadcasted_iota(I32, (LMAX, rows), 0)
        t_col = lax.broadcasted_iota(I32, (LMAX, rows), 1)
        me = lax.axis_index("dp")
        for j in range(group):
            target = peer(me, j, group)
            for r in range(slot_count):
                start, length = jnp.int32(0), jnp.int32(0)
                for p in range(prot_count):
                    hit = (dest_ref[p] == target) & (ranks[p] == r)
                    start = jnp.where(hit, starts[p], start)
                    length = jnp.where(hit, len_ref[p], length)
                chosen = (t_col == t_row + start) & (t_row < length)
                block = (j * slot_count + r) * LMAX
                sel_ref[block : block + LMAX, :] = chosen.astype(F32).astype(BF16)

    width = q_ref.shape[1]
    for h in range(width // HS):
        cols = slice(h * HS, (h + 1) * HS)
        scores = lax.dot_general(
            q_ref[:, cols], k_ref[:, cols], NT, preferred_element_type=F32
        ) * HS ** (-0.5)
        weights = jnp.where(mask_ref[...] > 0, jnp.exp(scores), 0.0)
        total = jnp.sum(weights, axis=1, keepdims=True)
        low = (weights / total).astype(BF16)
        spot = lanes_at(pl.program_id(0) * width + h * HS, HS)
        att_ref[:, spot] = jnp.dot(low, v_ref[:, cols], preferred_element_type=F32).astype(BF16)


def attention(projected, lengths, destination, group, slot_count):
    rows, width = projected.shape
    hidden = width // 3
    per = 4 * HS if hidden % (4 * HS) == 0 else HS
    steps = hidden // per
    sel_rows = group * slot_count * LMAX
    return pl.pallas_call(
        functools.partial(attention_kernel, lengths.shape[0], slot_count, group),
        grid_spec=pltpu.PrefetchScalarGridSpec(
            num_scalar_prefetch=2,
            grid=(steps,),
            in_specs=[
                pl.BlockSpec((rows, per), lambda i, *_: (0, i)),
                pl.BlockSpec((rows, per), lambda i, *_: (0, i + steps)),
                pl.BlockSpec((rows, per), lambda i, *_: (0, i + 2 * steps)),
            ],
            out_specs=[VMEM, VMEM],
            scratch_shapes=[pltpu.VMEM((rows, rows), F32)],
        ),
        out_shape=[pltpu.VMEM((rows, hidden), BF16), pltpu.VMEM((sel_rows, rows), BF16)],
        name="attention",
        compiler_params=SMALL,
    )(lengths, destination, projected, projected, projected)


def swap(x, axis, j):
    n = lax.axis_size(axis)
    pairs = [(i, int(i ^ j) if is_pow2(n) else (i + j) % n) for i in range(n)]
    return near(lax.ppermute(x, axis, pairs))


def rotate(x, axis):
    n = lax.axis_size(axis)
    return near(lax.ppermute(x, axis, [(i, (i + 1) % n) for i in range(n)]))


def add_kernel(*refs):
    terms, out = [r[...] for r in refs[:-1]], refs[-1]
    while len(terms) > 1:
        terms = [a + b for a, b in zip(terms[::2], terms[1::2])]
    out[...] = terms[0]


def add_up(terms):
    return near(
        pl.pallas_call(
            add_kernel,
            in_specs=[VMEM] * len(terms),
            out_specs=VMEM,
            out_shape=pltpu.VMEM(terms[0].shape, terms[0].dtype),
            name="add_up",
            compiler_params=SMALL,
        )(*terms)
    )


def my_share(cores):
    return lax.axis_index("parts") * cores + lax.rem(lax.axis_index("dp"), cores)


def shard_of(step, ring):
    return lax.rem(lax.axis_index("shard") + ring - step, ring)


def prepare_kernel(splits, cores, w_ref, *refs):
    *outs, held, sem = refs
    depth = held.shape[0]
    copy = pltpu.make_async_copy(
        w_ref.at[pl.ds(pl.multiple_of(my_share(cores) * depth, 16), depth), :], held, sem
    )
    copy.start()
    copy.wait()
    off = 0
    for out, width in zip(outs, splits):
        out[...] = held[:, off : off + width]
        off += width


def prepare(out_weight, splits, cores, depth):
    columns = out_weight.shape[1]
    return pl.pallas_call(
        functools.partial(prepare_kernel, splits, cores),
        in_specs=[ANY],
        out_specs=[VMEM] * len(splits),
        out_shape=[pltpu.VMEM((depth, w), BF16) for w in splits],
        scratch_shapes=[pltpu.VMEM((depth, columns), BF16), pltpu.SemaphoreType.DMA],
        name="prepare",
        compiler_params=SMALL,
    )(pltpu.with_memory_space_constraint(out_weight, pltpu.HBM))


def share_rows(count, cores, depth):
    mine = my_share(cores)
    return [r * depth for r in (mine, mine ^ cores, mine ^ 1, mine ^ cores ^ 1)][:count]


def first_probe_kernel(ring, columns, blocks, resid_ref, probe_ref, label_ref, *refs):
    hidden, (grad_ref, logits_ref) = refs[:-2], refs[-2:]
    tok_count = resid_ref.shape[0]
    logits = lax.dot_general(probe_ref[0], resid_ref[...], NT, preferred_element_type=F32)
    mismatch = mismatch_of(logits, label_ref[...], tok_count)
    grad_ref[...] = jnp.dot(mismatch, resid_ref[...], preferred_element_type=F32)
    logits_ref[...] = partial_logits(ring, columns, blocks, probe_ref, hidden)


def partial_logits(ring, columns, blocks, probe_ref, hidden):
    total = None
    for (step, off, width), rows in zip(blocks, hidden):
        probe = probe_ref[1, :, lanes_at(shard_of(step, ring) * columns + off, width)]
        part = lax.dot_general(probe, rows[...], NT, preferred_element_type=F32)
        total = part if total is None else total + part
    return total


def first_probe(blocks, residual, probes, label_row, hidden, ring, columns):
    rows, width = residual.shape
    return pl.pallas_call(
        functools.partial(first_probe_kernel, ring, columns, blocks),
        in_specs=[VMEM] * (3 + len(hidden)),
        out_specs=[VMEM] * 2,
        out_shape=[pltpu.VMEM((CLASSES, width), F32), pltpu.VMEM((CLASSES, rows), F32)],
        name="first_probe",
        compiler_params=SMALL,
    )(residual, probes, label_row, *hidden)


def second_probe_kernel(group, ring, columns, blocks, known, probe_ref, label_ref, grad_ref, logits_ref, *refs):
    hidden, outs, grads = refs[: len(blocks)], refs[len(blocks) : -1], refs[-1]
    tok_count = label_ref.shape[1]
    rest = partial_logits(ring, columns, blocks[known:], probe_ref, hidden[known:])
    mismatch = mismatch_of(logits_ref[...] + rest, label_ref[...], tok_count)
    grads[0:CLASSES, :] = grad_ref[...]
    for (step, off, width), rows in zip(blocks, hidden):
        spot = lanes_at(shard_of(step, ring) * columns + off, width)
        grads[CLASSES:, spot] = jnp.dot(mismatch, rows[...], preferred_element_type=F32)
    me = lax.axis_index("dp")
    for j, out in enumerate(outs):
        width = out.shape[1]
        out[...] = grads[:, lanes_at(peer(me, j, group) * width, width)]


def second_probe(blocks, known, probes, label_row, first, logits, hidden, group, ring, columns):
    width = first.shape[1]
    return pl.pallas_call(
        functools.partial(second_probe_kernel, group, ring, columns, blocks, known),
        in_specs=[VMEM] * (4 + len(hidden)),
        out_specs=[VMEM] * group,
        out_shape=[pltpu.VMEM((2 * CLASSES, width // group), F32)] * group,
        scratch_shapes=[pltpu.VMEM((2 * CLASSES, width), F32)],
        name="second_probe",
        compiler_params=SMALL,
    )(probes, label_row, first, logits, *hidden)


def gradient_kernel(group, *refs):
    pieces, out_ref = refs[:-1], refs[-1]
    me = lax.axis_index("dp")
    width = pieces[0].shape[1]
    for j, piece in enumerate(pieces):
        spot = lanes_at(peer(me, j, group) * width, width)
        out_ref[0, :, spot] = piece[0:CLASSES, :]
        out_ref[1, :, spot] = piece[CLASSES:, :]


def gradient(pieces):
    group = len(pieces)
    return pl.pallas_call(
        functools.partial(gradient_kernel, group),
        in_specs=[VMEM] * group,
        out_specs=VMEM,
        out_shape=jax.ShapeDtypeStruct((2, CLASSES, group * pieces[0].shape[1]), F32),
        name="gradient",
        compiler_params=SMALL,
    )(*pieces)


def project_kernel(blocks, group, ring, cores, columns, att_ref, resid_ref, sel_ref, *refs):
    pieces, sends, hid_ref = refs[: -group - 1], refs[-group - 1 : -1], refs[-1]
    span = sel_ref.shape[0] // group
    done, at = 0, 0
    for step, off, width, count in blocks:
        depth = pieces[done].shape[0]
        total = None
        for row, piece in zip(share_rows(count, cores, depth), pieces[done : done + count]):
            rows = att_ref[...] if count == 1 else att_ref[:, lanes_at(row, depth)]
            part = jnp.dot(rows, piece[...], preferred_element_type=F32)
            total = part if total is None else total + part
        resid = resid_ref[:, lanes_at(shard_of(step, ring) * columns + off, width)]
        hidden = (total + resid.astype(F32)).astype(BF16)
        hid_ref[:, at : at + width] = hidden
        for j, send in enumerate(sends):
            send[:, at : at + width] = jnp.dot(
                sel_ref[j * span : (j + 1) * span, :], hidden, preferred_element_type=F32
            ).astype(BF16)
        done += count
        at += width


def project(blocks, att, residual, sel, pieces, group, ring, cores, columns):
    span = sel.shape[0] // group
    width = sum(w for _, _, w, _ in blocks)
    return pl.pallas_call(
        functools.partial(project_kernel, blocks, group, ring, cores, columns),
        in_specs=[VMEM] * (3 + len(pieces)),
        out_specs=[VMEM] * (group + 1),
        out_shape=[pltpu.VMEM((span, width), BF16)] * group + [pltpu.VMEM((att.shape[0], width), BF16)],
        name="project",
        compiler_params=SMALL,
    )(att, residual, sel, *pieces)


def place_kernel(sets, group, ring, columns, *refs):
    blocks, out_ref, sems = refs[: group * len(sets)], refs[-2], refs[-1]
    me = lax.axis_index("dp")
    stores = []
    for s, (step, off, width) in enumerate(sets):
        for j in range(group):
            block = blocks[s * group + j]
            span = block.shape[0]
            stores.append(
                pltpu.make_async_copy(
                    block,
                    out_ref.at[
                        pl.ds(pl.multiple_of(source(me, j, group) * span, 16), span),
                        lanes_at(shard_of(step, ring) * columns + off, width),
                    ],
                    sems.at[len(stores)],
                )
            )
    for store in stores:
        store.start()
    for store in stores:
        store.wait()


def place(sets, blocks, out, shape, group, ring, columns):
    held = [] if out is None else [out]
    return pl.pallas_call(
        functools.partial(place_kernel, sets, group, ring, columns),
        in_specs=[VMEM] * len(blocks) + [ANY] * len(held),
        out_specs=ANY,
        out_shape=jax.ShapeDtypeStruct(shape, BF16),
        scratch_shapes=[pltpu.SemaphoreType.DMA((len(blocks),))],
        input_output_aliases={len(blocks): 0} if held else {},
        name="place",
        compiler_params=SMALL,
    )(*blocks, *held)


def splits_of(columns):
    whole = sum(PARTS_OF_COLUMNS) * LANES
    if columns % whole:
        return (columns,)
    return tuple(columns // sum(PARTS_OF_COLUMNS) * p for p in PARTS_OF_COLUMNS)


def is_fast(mesh_shape, columns, inner):
    parts, group, ring = mesh_shape["parts"], mesh_shape["dp"], mesh_shape["shard"]
    if (parts, group, ring) != (2, 4, 4):
        return False
    return len(splits_of(columns)) == 2 and inner % (parts * 2 * LANES) == 0


def per_device_fast(projected, residual, out_weight, probe_weight, labels, lengths, destination):
    group, ring = lax.axis_size("dp"), lax.axis_size("shard")
    cores = 2
    slot_count = -(-lengths.shape[1] // group)
    inner, columns = out_weight.shape
    splits = splits_of(columns)
    offs = (0, splits[0])
    depth = inner // (2 * cores)
    shape = (group * slot_count * LMAX, residual.shape[1])
    probes = jnp.swapaxes(probe_weight, 1, 2)
    label_row = labels.reshape(1, -1)

    def fill(piece):
        other = swap(piece, "parts", 1)
        return [piece, other, swap(piece, "dp", 1), swap(other, "dp", 1)]

    def send(made):
        *sends, hid = [near(m) for m in made]
        hidden.append(hid)
        return [sends[0]] + [swap(sends[j], "dp", j) for j in range(1, group)]

    def chunk(step, i, count=4):
        return (step, offs[i], splits[i], count)

    tail = (group, ring, cores, columns)
    hidden = []
    held = [near(h) for h in prepare(out_weight, splits, cores, depth)]
    att, sel = map(near, attention(projected, lengths[0], destination[0], group, slot_count))
    residual, weight_here = near(residual), near(out_weight)

    ring_a, ring_b = [held[0]], [held[1]]
    for _ in range(1, ring):
        ring_a.append(rotate(ring_a[-1], "shard"))
        ring_b.append(rotate(ring_b[-1], "shard"))
    chunks = [[fill(ring_a[s]), fill(ring_b[s])] if s else None for s in range(ring)]
    made = project(((0, 0, columns, 1),), att, residual, sel, [weight_here], *tail)
    got0 = send(made)
    made = project((chunk(1, 0), chunk(1, 1)), att, residual, sel, chunks[1][0] + chunks[1][1], *tail)
    got1 = send(made)
    made = project((chunk(2, 0), chunk(2, 1)), att, residual, sel, chunks[2][0] + chunks[2][1], *tail)
    got2 = send(made)
    made = project((chunk(3, 0),), att, residual, sel, chunks[3][0], *tail)
    got3 = send(made)
    made = project((chunk(3, 1),), att, residual, sel, chunks[3][1], *tail)
    got4 = send(made)

    early = tuple((step, 0, columns) for step in range(3))
    late = tuple((3, off, width) for off, width in zip(offs, splits))
    known = len(early) + 1
    first, logits = map(
        near,
        first_probe((early + late)[:known], residual, probes, label_row, hidden[:known], ring, columns),
    )
    cuts = second_probe(
        early + late, known, probes, label_row, first, logits, hidden, group, ring, columns
    )
    cuts = [near(c) for c in cuts]
    total = add_up([cuts[0]] + [swap(cuts[j], "dp", j) for j in range(1, group)])
    for j in (1, 2):
        total = add_up([total, swap(total, "shard", j)])
    grads = gradient([total] + [swap(total, "dp", j) for j in range(1, group)])

    where = (group, ring, columns)
    out = place(early, got0 + got1 + got2, None, shape, *where)
    out = place(late, got3 + got4, out, shape, *where)
    return out, jnp.swapaxes(grads, 1, 2)


def general_probe_kernel(tok_count, label_ref, probe_ref, chunk_ref, grad_ref):
    chunk = chunk_ref[...]
    logits = lax.dot_general(probe_ref[...], chunk, NT, preferred_element_type=F32)
    mismatch = mismatch_of(logits, label_ref[...], tok_count)
    grad_ref[...] = jnp.dot(mismatch, chunk, preferred_element_type=F32)


def general_probe(label_row, probe, represent):
    return pl.pallas_call(
        functools.partial(general_probe_kernel, label_row.shape[1]),
        in_specs=[VMEM] * 3,
        out_specs=VMEM,
        out_shape=jax.ShapeDtypeStruct(probe.shape, F32),
        name="probe",
    )(label_row, probe, represent)


def per_device_general(projected, residual, out_weight, probe_weight, labels, lengths, destination):
    group, ring = lax.axis_size("dp"), lax.axis_size("shard")
    me, z = lax.axis_index("dp"), lax.axis_index("shard")
    slot_count = -(-lengths.shape[1] // group)
    columns = out_weight.shape[1]
    hidden_width = residual.shape[1]
    att, sel = attention(projected, lengths[0], destination[0], group, slot_count)
    hidden = jnp.zeros(residual.shape, BF16)
    held = out_weight
    for step in range(ring):
        if step:
            held = lax.ppermute(held, "shard", [(i, (i + 1) % ring) for i in range(ring)])
        col = lax.rem(z + ring - step, ring) * columns
        resid = lax.dynamic_slice(residual, (0, col), (residual.shape[0], columns))
        mixed = jnp.dot(att, held, preferred_element_type=F32) + resid.astype(F32)
        hidden = lax.dynamic_update_slice(hidden, mixed.astype(BF16), (0, col))
    label_row = labels.reshape(1, -1)
    probes = jnp.swapaxes(probe_weight, 1, 2)
    grads = [general_probe(label_row, probes[k], r) for k, r in enumerate((residual, hidden))]
    grads = lax.psum(jnp.stack(grads), ("dp", "shard"))
    packed = jnp.dot(sel, hidden, preferred_element_type=F32).astype(BF16)
    packed = packed.reshape(group, slot_count * LMAX, hidden_width)
    places = jnp.arange(group, dtype=I32)
    spots = places ^ me if is_pow2(group) else lax.rem(places + group - me, group)
    packed = jnp.take(packed, spots, axis=0)
    packed = lax.all_to_all(packed, "dp", split_axis=0, concat_axis=0, tiled=True)
    return packed.reshape(-1, hidden_width), jnp.swapaxes(grads, 1, 2)


def solution(mesh):
    def per_device(projected, residual, out_weight, *rest):
        fast = is_fast(dict(mesh.shape), out_weight.shape[1], out_weight.shape[0])
        body = per_device_fast if fast else per_device_general
        return body(projected, residual, out_weight, *rest)

    return jax.shard_map(
        per_device,
        mesh=mesh,
        in_specs=(
            P(("parts", "dp", "shard"), None),
            P(("parts", "dp", "shard"), None),
            P(None, "shard"),
            P(),
            P(("parts", "dp", "shard")),
            P(("parts", "dp", "shard"), None),
            P(("parts", "dp", "shard"), None),
        ),
        out_specs=(P(("parts", "dp", "shard"), None), P("parts", None, None)),
        check_vma=False,
    )
```
